32 devices in a mesh: scene: 2 (over x), mrow: 8 (over z, y), mcol: 2 (over core).
Axes of the slice: x: 2, y: 2, z: 4, core: 2. Of those that a mesh axis runs over, the one named last changes fastest.
Arguments:
- pan_blocks: bfloat16 [2048, 128, 128], P(('scene', 'mrow', 'mcol')), parts along dimension 0, may hold values from -6 to 6
- ms_blocks: bfloat16 [2048, 32, 256], P(('scene', 'mrow', 'mcol')), parts along dimension 0, may hold values from -6 to 6
- send_list: int32 [3, 2048], P(None, ('scene', 'mrow', 'mcol')), parts along dimension 1, may hold values from 0 to 127, as said below
- tile_list: int32 [3, 4096], P(None, ('scene', 'mrow', 'mcol')), parts along dimension 1, may hold values from 0 to 9, as said below
- row_grid: float32 [48], P(('scene', 'mrow')), parts along dimension 0, may hold values from -32 to 288
- col_grid: float32 [16, 16], P(('scene', 'mrow'), 'mcol'), parts along dimension 0, may hold values from -32 to 1312
- band_mix: float32 [8, 8], replicated, may hold values from -1.5 to 1.5
- band_gain: float32 [8], replicated, may hold values from 0.4 to 1.2
- synth_weight: float32 [8], replicated, may hold values from 0.05 to 0.3
Outputs:
- sharpened: bfloat16 [8, 2048, 1024], P(None, ('scene', 'mrow'), 'mcol'), parts along dimension 1
The draws below stay inside these ranges and needn't reach their ends.
There are 2 independent parts, one for each index of `scene`. The reference program is written for one: setup_inputs(seed, part) draws one part's arguments, and reference() takes and returns one part's arrays. A program takes and returns all parts, laid end to end along the dimension named above; an argument that names none is the same for every part. Nothing has to cross between parts.
Inputs may be any that keep to these rules, and one draw needn't show every extreme that they name: `send_list`: row 0 gives each source block of a device a distinct send slot; slot p goes to map-row owner p // 16 in the device's own map column, so one device sends at most 16 blocks to one tile; in every draw one tile of each map column receives 16 blocks from every device of that column, and every device fills 16 slots of it. Row 1 is a cell row below 2; row 2 a cell column between mcol * 5 and mcol * 5 + 4. `tile_list`: row 0 is 1 exactly in the receive slots that send_list fills and 0 elsewhere; rows 1 and 2 repeat the cell row and column of the block sent there, and are 0 in empty slots.
All inputs are finite; a program needn't handle non-finite values.
Results may differ from the reference program's by a relative error of at most 0.0073.
Values may be sent and summed in bfloat16 or wider, within the bound.
A program may use at most 128 MiB of HBM per device.

```python
import math
import jax
import jax.numpy as jnp
from jax import lax

BANDS = 8
BS = 128
GRID = 64
TR = 128
TC = 512
SBD = 64
MB = 32
KR = 2
KC = 5
NR = 1024
NC = 1024
N_MROW = 8
N_MCOL = 2


def route_tables(key):
    devices = N_MROW * N_MCOL
    partition_total = 2 * SBD
    capacity = partition_total // N_MROW
    stochastic_seed_sequence = jax.random.split(jax.random.fold_in(key, 4242), 6)
    favoured = jax.random.randint(stochastic_seed_sequence[0], (N_MCOL,), 0, N_MROW)
    preference_extra_digits = jax.random.randint(stochastic_seed_sequence[1], (N_MCOL, N_MROW), 0, 4)
    stochastic_perturb_digits = jax.random.randint(stochastic_seed_sequence[2], (devices, partition_total), 0, 1024)
    partition_number = jnp.arange(partition_total, dtype=jnp.int32)
    keeper_line = partition_number // capacity
    horizontal_location = jnp.arange(devices, dtype=jnp.int32) % N_MCOL
    reached_capacity_flag = (keeper_line[None, :] == jnp.take(favoured, horizontal_location)[:, None]).astype(jnp.int32)
    preference_extra_order = jnp.take(jnp.take(preference_extra_digits, horizontal_location, axis=0), keeper_line, axis=1)
    preference_grades = ((reached_capacity_flag * 8 + preference_extra_order) * 1024 + stochastic_perturb_digits) * partition_total + partition_number[None, :]
    top_scores, chosen = lax.top_k(preference_grades, SBD)
    shuffle = jax.random.randint(stochastic_seed_sequence[5], (devices, SBD), 0, 4096) * SBD + jnp.arange(SBD, dtype=jnp.int32)[None, :]
    reorder = jnp.argsort(shuffle, axis=1)
    chosen = jnp.take_along_axis(chosen, reorder, axis=1).astype(jnp.int32)
    cell_rows = jax.random.randint(stochastic_seed_sequence[3], (devices, SBD), 0, KR)
    cell_cols = horizontal_location[:, None] * KC + jax.random.randint(stochastic_seed_sequence[4], (devices, SBD), 0, KC)
    flat_slots = chosen.reshape(-1)
    sender = jnp.repeat(jnp.arange(devices, dtype=jnp.int32), SBD)
    destination = (flat_slots // capacity * N_MCOL + sender % N_MCOL) * partition_total + sender // N_MCOL * capacity + flat_slots % capacity
    entries = jnp.stack([jnp.ones_like(flat_slots), cell_rows.reshape(-1), cell_cols.reshape(-1)]).astype(jnp.int32)
    tile_table = jnp.zeros((3, devices * partition_total), jnp.int32).at[:, destination].set(entries)
    send_table = jnp.stack([flat_slots, cell_rows.reshape(-1), cell_cols.reshape(-1)]).astype(jnp.int32)
    return (send_table, tile_table)


def draw_send_list(key, part):
    return route_tables(key)[0]


def draw_tile_list(key, part):
    return route_tables(key)[1]


def draw_row_grid(key, part):
    node_count = TR // GRID + 1
    stochastic_seed_sequence = jax.random.split(jax.random.fold_in(key, 11), 3)
    reach = float(KR * BS)
    lead_gap = jax.random.uniform(stochastic_seed_sequence[0], (N_MROW, 1), minval=1.0, maxval=6.0)
    tail_gap = jax.random.uniform(stochastic_seed_sequence[1], (N_MROW, 1), minval=1.0, maxval=6.0)
    shake = 0.15
    fraction = jnp.arange(node_count, dtype=jnp.int32).astype(jnp.float32) / (node_count - 1)
    jitter = jax.random.uniform(stochastic_seed_sequence[2], (N_MROW, node_count), minval=-1.0, maxval=1.0) * (shake * GRID)
    nodes_all = lead_gap + (reach - lead_gap - tail_gap) * fraction[None, :] + jitter
    return nodes_all.reshape(-1).astype(jnp.float32)


def draw_col_grid(key, part):
    node_count = NC // GRID
    stochastic_seed_sequence = jax.random.split(jax.random.fold_in(key, 23), 3)
    reach = float(N_MCOL * KC * BS)
    lead_gap = jax.random.uniform(stochastic_seed_sequence[0], (N_MROW, 1), minval=1.0, maxval=6.0)
    tail_gap = jax.random.uniform(stochastic_seed_sequence[1], (N_MROW, 1), minval=1.0, maxval=6.0)
    shake = 0.15
    fraction = (GRID * jnp.arange(node_count, dtype=jnp.int32)).astype(jnp.float32) / NC
    jitter = jax.random.uniform(stochastic_seed_sequence[2], (N_MROW, node_count), minval=-1.0, maxval=1.0) * (shake * GRID)
    return (lead_gap + (reach - lead_gap - tail_gap) * fraction[None, :] + jitter).astype(jnp.float32)


def shard_levels(own_key, extent, shards, smallest, high):
    gain = 1.0
    for dim, shards_of in shards:
        heights = jax.random.uniform(jax.random.fold_in(jax.random.fold_in(own_key, 6), dim), (shards_of,), jnp.float32, smallest / len(shards), high / len(shards))
        gain = gain * jnp.repeat(jnp.exp(heights), extent[dim] // shards_of).reshape((-1,) + (1,) * (len(extent) - 1 - dim))
    return gain


def bell_draw(stream_key, shape, spread, most, pieces=(), kind=jnp.bfloat16):
    values = jax.random.normal(stream_key, shape, jnp.float32) * spread
    if len(pieces) > 0:
        values = shard_levels(stream_key, shape, pieces, -0.22, 0.18) * values
    return jnp.clip(values, min=-most, max=most).astype(kind)


def setup_inputs(seed: int = 0, part: int = 0) -> dict:
    streams_of = jax.random.split(jax.random.key(seed), 10)
    part_splits = jax.random.split(jax.random.fold_in(streams_of[9], part), 10)
    return {
        "pan_blocks": bell_draw(part_splits[0], (N_MROW * N_MCOL * SBD, BS, BS), 1.0, 6.0, ((0, 16),)),
        "ms_blocks": bell_draw(part_splits[1], (N_MROW * N_MCOL * SBD, MB, BANDS * MB), 1.0, 6.0, ((0, 16),)),
        "send_list": draw_send_list(jax.random.fold_in(jax.random.fold_in(streams_of[9], part), 71), part),
        "tile_list": draw_tile_list(jax.random.fold_in(jax.random.fold_in(streams_of[9], part), 71), part),
        "row_grid": draw_row_grid(jax.random.fold_in(jax.random.fold_in(streams_of[9], part), 71), part),
        "col_grid": draw_col_grid(jax.random.fold_in(jax.random.fold_in(streams_of[9], part), 71), part),
        "band_mix": bell_draw(streams_of[6], (BANDS, BANDS), 0.3, 1.5, (), jnp.float32),
        "band_gain": jnp.clip(jax.random.uniform(streams_of[7], (BANDS,), jnp.float32, 0.4, 1.2), 0.4, 1.2),
        "synth_weight": jnp.clip(jnp.exp(jax.random.uniform(streams_of[8], (BANDS,), jnp.float32, math.log(0.05), math.log(0.3))), 0.05, 0.3),
    }


highest = lax.Precision.HIGHEST


def cubic_weight(offset):
    distance = jnp.abs(offset)
    near_part = (1.5 * distance - 2.5) * distance * distance + 1.0
    far_part = ((-0.5 * distance + 2.5) * distance - 4.0) * distance + 2.0
    return jnp.where(distance <= 1.0, near_part, jnp.where(distance < 2.0, far_part, jnp.zeros_like(distance)))


def along_nodes(node_values, position, offset, spacing):
    segment = jnp.minimum(position // spacing, node_values.shape[-1] - 2)
    left_node = jnp.take(node_values, segment, axis=-1)
    right_node = jnp.take(node_values, segment + 1, axis=-1)
    within = ((position - segment * spacing).astype(jnp.float32) + offset) / spacing
    return left_node + (right_node - left_node) * within


def source_weights(coords, cell_ids, block_size):
    pixels = (cell_ids[:, None, None] * block_size + jnp.arange(block_size, dtype=jnp.int32)[None, None, :]).astype(jnp.float32)
    return cubic_weight(coords[:, :, None] - pixels).astype(jnp.bfloat16)


def row_weights(coords, cell_ids, is_valid, block_size):
    pixels = (cell_ids[None, :, None] * block_size + jnp.arange(block_size, dtype=jnp.int32)[None, None, :]).astype(jnp.float32)
    return (cubic_weight(coords[:, None, None] - pixels) * is_valid[None, :, None]).astype(jnp.bfloat16)


def upsample_table(length, coarse):
    position = (jnp.arange(length, dtype=jnp.int32).astype(jnp.float32) - 1.5) * 0.25 + 2.0
    taps = jnp.arange(coarse + 4, dtype=jnp.int32).astype(jnp.float32)
    return cubic_weight(position[:, None] - taps[None, :]).astype(jnp.bfloat16)


def combine(upsampled, pan_map, band_mix, band_gain, synth_weight):
    mixture = jnp.transpose(upsampled, (1, 0, 2)) + jnp.einsum("bk,rkc->brc", band_mix, upsampled, precision=highest)
    synthetic = jnp.einsum("k,rkc->rc", synth_weight, upsampled, precision=highest)
    return (mixture + band_gain[:, None, None] * (pan_map - synthetic)[None, :, :]).astype(jnp.bfloat16)


def reference(pan_blocks, ms_blocks, send_list, tile_list, row_grid, col_grid, band_mix, band_gain, synth_weight):
    devices = N_MROW * N_MCOL
    partition_total = 2 * SBD
    capacity = partition_total // N_MROW
    node_count = TR // GRID + 1
    coarse_rows = TR // 4
    coarse_cols = TC // 4
    block_ids = jnp.arange(devices * SBD, dtype=jnp.int32)
    sender = block_ids // SBD
    partition_number = send_list[0]
    target = ((partition_number // capacity) * N_MCOL + sender % N_MCOL) * partition_total + (sender // N_MCOL) * capacity + partition_number % capacity
    receive = jnp.zeros((devices * partition_total,), jnp.int32).at[target].set(block_ids)

    def one_tile(device):
        row_band = device // N_MCOL
        horizontal_location = device % N_MCOL
        slot_index = lax.dynamic_slice_in_dim(receive, device * partition_total, partition_total)
        tile_lists = lax.dynamic_slice_in_dim(tile_list, device * partition_total, partition_total, 1)
        is_valid = tile_lists[0].astype(jnp.float32)
        cell_rows = tile_lists[1]
        cell_cols = tile_lists[2]
        pan_data = jnp.take(pan_blocks, slot_index, axis=0).astype(jnp.float32)
        ms_data = jnp.take(ms_blocks, slot_index, axis=0).astype(jnp.float32).reshape(partition_total, MB, BANDS, MB)
        row_nodes = lax.dynamic_slice_in_dim(row_grid, row_band * node_count, node_count)
        col_nodes = lax.dynamic_index_in_dim(col_grid, row_band, 0, False)
        map_rows = jnp.arange(TR, dtype=jnp.int32)
        map_cols = horizontal_location * TC + jnp.arange(TC, dtype=jnp.int32)
        y_pan = along_nodes(row_nodes, map_rows, 0.0, GRID)
        x_pan = along_nodes(col_nodes, map_cols, 0.0, GRID)
        y_ms = (along_nodes(row_nodes, 4 * jnp.arange(coarse_rows, dtype=jnp.int32) + 1, 0.5, GRID) - 1.5) * 0.25
        x_ms = (along_nodes(col_nodes, horizontal_location * TC + 4 * jnp.arange(coarse_cols, dtype=jnp.int32) + 1, 0.5, GRID) - 1.5) * 0.25
        col_weight = source_weights(x_pan[None, :], cell_cols, BS)
        pan_cols = jnp.einsum("sij,scj->sic", pan_data, col_weight.astype(jnp.float32), precision=highest).astype(jnp.bfloat16)
        row_weight = row_weights(y_pan, cell_rows, is_valid, BS)
        pan_map = jnp.dot(row_weight.reshape(TR, partition_total * BS), pan_cols.reshape(partition_total * BS, TC), preferred_element_type=jnp.float32)
        ms_col_weight = source_weights(x_ms[None, :], cell_cols, MB)
        ms_cols = jnp.einsum("sibj,scj->sibc", ms_data, ms_col_weight.astype(jnp.float32), precision=highest).astype(jnp.bfloat16)
        ms_row_weight = row_weights(y_ms, cell_rows, is_valid, MB)
        ms_map = jnp.dot(ms_row_weight.reshape(coarse_rows, partition_total * MB), ms_cols.reshape(partition_total * MB, BANDS * coarse_cols), preferred_element_type=jnp.float32).astype(jnp.bfloat16)
        return pan_map, ms_map.reshape(coarse_rows, BANDS, coarse_cols)

    pan_maps, ms_maps = lax.map(one_tile, jnp.arange(devices, dtype=jnp.int32))
    strip_map = ms_maps.reshape(N_MROW, N_MCOL, coarse_rows, BANDS, coarse_cols).transpose(0, 2, 3, 1, 4).reshape(N_MROW * coarse_rows, BANDS, N_MCOL * coarse_cols)
    padded = jnp.pad(strip_map, ((2, 2), (0, 0), (2, 2)))
    up_rows = upsample_table(TR, coarse_rows)
    up_cols = upsample_table(TC, coarse_cols)

    def sharpen(device):
        row_band = device // N_MCOL
        horizontal_location = device % N_MCOL
        window = lax.dynamic_slice(padded, (row_band * coarse_rows, jnp.zeros((), jnp.int32), horizontal_location * coarse_cols), (coarse_rows + 4, BANDS, coarse_cols + 4))
        across = jnp.einsum("mbn,cn->mbc", window.astype(jnp.float32), up_cols.astype(jnp.float32), precision=highest).astype(jnp.bfloat16)
        upsampled = jnp.dot(up_rows, across.reshape(coarse_rows + 4, BANDS * TC), preferred_element_type=jnp.float32).reshape(TR, BANDS, TC)
        pan_map = lax.dynamic_index_in_dim(pan_maps, device, 0, False)
        return combine(upsampled, pan_map, band_mix, band_gain, synth_weight)

    tiles = lax.map(sharpen, jnp.arange(devices, dtype=jnp.int32))
    return tiles.reshape(N_MROW, N_MCOL, BANDS, TR, TC).transpose(2, 0, 3, 1, 4).reshape(BANDS, NR, NC)
```

```python
import functools

import jax
import jax.numpy as jnp
from jax import lax
from jax.experimental import pallas as pl
from jax.experimental.pallas import tpu as pltpu
from jax.sharding import PartitionSpec as P

GRID = 64
TR = 128
TC = 512
KR = 2
KC = 5
MESH = pl.DeviceIdType.MESH
F32 = jnp.float32
BF16 = jnp.bfloat16


def cubic_weight(offset):
    distance = jnp.abs(offset)
    near_part = (1.5 * distance - 2.5) * distance * distance + 1.0
    far_part = ((-0.5 * distance + 2.5) * distance - 4.0) * distance + 2.0
    return jnp.where(
        distance <= 1.0, near_part, jnp.where(distance < 2.0, far_part, jnp.zeros_like(distance))
    )


def iota(shape, dim):
    return lax.broadcasted_iota(jnp.int32, shape, dim)


def cell_sums(capacity, send_ref, pan_ref, ms_ref, pan_out, ms_out, slot_block, pan_acc, ms_acc):
    tile = pl.program_id(0)
    own_blocks, block_size, _ = pan_ref.shape
    _, coarse_size, coarse_width = ms_ref.shape
    first_col = lax.axis_index("mcol") * KC

    @pl.when(tile == 0)
    def _():
        def clear(slot, carry):
            slot_block[slot] = -1
            return carry

        lax.fori_loop(0, slot_block.shape[0], clear, 0)

        def enter(block, carry):
            slot_block[send_ref[0, block]] = block
            return carry

        lax.fori_loop(0, own_blocks, enter, 0)

    pan_acc[...] = jnp.zeros_like(pan_acc)
    ms_acc[...] = jnp.zeros_like(ms_acc)

    def add(slot, carry):
        block = slot_block[tile * capacity + slot]

        @pl.when(block >= 0)
        def _():
            row = send_ref[1, block]
            col = send_ref[2, block] - first_col
            at = (
                pl.ds(pl.multiple_of(row * block_size, block_size), block_size),
                pl.ds(pl.multiple_of(col * block_size, block_size), block_size),
            )
            pan_acc[at] += pan_ref[block].astype(F32)
            at = (
                pl.ds(pl.multiple_of(row * coarse_size, coarse_size), coarse_size),
                pl.ds(pl.multiple_of(col * coarse_width, coarse_width), coarse_width),
            )
            ms_acc[at] += ms_ref[block].astype(F32)

        return carry

    lax.fori_loop(0, capacity, add, 0)
    pan_out[0] = pan_acc[...].astype(BF16)
    ms_out[0] = ms_acc[...].astype(BF16)


def row_coord(nodes, position, offset):
    first = position < GRID
    a = jnp.where(first, nodes[0:1, 0:1], nodes[0:1, 1:2])
    b = jnp.where(first, nodes[0:1, 1:2], nodes[0:1, 2:3])
    within = (jnp.where(first, position, position - GRID).astype(F32) + offset) / GRID
    return a + (b - a) * within


def col_coord(nodes, after, is_last, count, position, offset):
    segment = position // GRID
    coord = jnp.zeros(position.shape, F32)
    for s in range(count):
        left, shift = nodes[1:2, s : s + 1], s * GRID
        if s + 1 < count:
            right = nodes[1:2, s + 1 : s + 2]
        else:
            right = jnp.where(is_last, left, after)
            left = jnp.where(is_last, nodes[1:2, s - 1 : s], left)
            shift = jnp.where(is_last, shift - GRID, shift)
        within = ((position - shift).astype(F32) + offset) / GRID
        coord = jnp.where(segment == s, left + (right - left) * within, coord)
    return coord


def mapping(
    col_nodes,
    nodes_ref,
    pan_ref,
    ms_ref,
    mix_ref,
    gain_ref,
    out_ref,
    nodes_all,
    nodes_beside,
    pair_send,
    pair_recv,
    owner_send,
    owner_recv,
    total,
    col_weight,
    ms_col_weight,
    window,
    beside,
    up_cols,
    up_rows,
    pan_map,
    upsampled,
    nodes_ss,
    nodes_rs,
    pair_ss,
    pair_rs,
    owner_ss,
    owner_rs,
    halo_ss,
    halo_rs,
):
    n = lax.axis_size("mrow")
    pairs = n // 2
    scene = lax.axis_index("scene")
    m = lax.axis_index("mrow")
    c = lax.axis_index("mcol")
    z, y = m // 2, m % 2
    twin = z * 2 + (1 - y)
    other = 1 - c
    cols = pan_ref.shape[2]
    pan_rows = pan_ref.shape[1]
    ms_rows = ms_ref.shape[1]
    bands = out_ref.shape[0]
    coarse_rows = TR // 4
    coarse_cols = TC // 4
    half = coarse_rows // 2
    coarse_size = ms_rows // KR

    def at(row, col):
        return (scene, row, col)

    barrier = pltpu.get_barrier_semaphore()

    def greet(k, carry):
        row = lax.rem(m + k, n)
        pl.semaphore_signal(barrier, inc=1, device_id=at(row, c), device_id_type=MESH)
        pl.semaphore_signal(barrier, inc=1, device_id=at(row, other), device_id_type=MESH)
        return carry

    pl.semaphore_signal(barrier, inc=1, device_id=at(m, other), device_id_type=MESH)
    lax.fori_loop(1, n, greet, 0)
    pl.semaphore_wait(barrier, 2 * n - 1)

    def nodes_copy(slot, row):
        return pltpu.make_async_remote_copy(
            src_ref=nodes_ref,
            dst_ref=nodes_all.at[slot],
            send_sem=nodes_ss.at[row],
            recv_sem=nodes_rs.at[slot],
            device_id=at(row, c),
            device_id_type=MESH,
        )

    beside_copy = pltpu.make_async_remote_copy(
        src_ref=nodes_ref,
        dst_ref=nodes_beside,
        send_sem=nodes_ss.at[n],
        recv_sem=nodes_rs.at[n],
        device_id=at(m, other),
        device_id_type=MESH,
    )

    def send_nodes(k, carry):
        nodes_copy(m, lax.rem(m + k, n)).start()
        return carry

    lax.fori_loop(1, n, send_nodes, 0)
    beside_copy.start()
    nodes_all[m] = nodes_ref[...]

    tap = iota((TR, 2 * coarse_rows), 1) - (half - 2)
    spot = (iota((TR, 2 * coarse_rows), 0).astype(F32) - 1.5) * 0.25 + 2.0
    up_rows[...] = cubic_weight(spot - tap.astype(F32)).astype(BF16)
    spot = (iota((coarse_cols, TC), 1).astype(F32) - 1.5) * 0.25 + 2.0
    tap = iota((coarse_cols, TC), 0) + 2
    up_cols[0] = cubic_weight(spot - tap.astype(F32)).astype(BF16)
    tap = tap + jnp.where(c == 0, coarse_cols, -coarse_cols)
    up_cols[1] = cubic_weight(spot - tap.astype(F32)).astype(BF16)

    def wait_nodes(k, carry):
        row = lax.rem(m + k, n)
        nodes_copy(row, row).wait()
        return carry

    lax.fori_loop(1, n, wait_nodes, 0)
    beside_copy.wait()

    def row_pass(tile):
        nodes = nodes_all[tile]
        shape = (TR, pan_rows)
        weight = cubic_weight(
            row_coord(nodes, iota(shape, 0), 0.0) - iota(shape, 1).astype(F32)
        ).astype(BF16)
        pan = jnp.dot(weight, pan_ref[tile], preferred_element_type=F32)
        shape = (coarse_rows, ms_rows)
        spots = (row_coord(nodes, 4 * iota(shape, 0) + 1, 0.5) - 1.5) * 0.25
        weight = cubic_weight(spots - iota(shape, 1).astype(F32)).astype(BF16)
        left = jnp.dot(weight, ms_ref[tile, :, 0:cols], preferred_element_type=F32)
        right = jnp.dot(weight, ms_ref[tile, :, cols : 2 * cols], preferred_element_type=F32)
        return pan, left, right

    pieces = (
        slice(0, TR),
        slice(TR, TR + coarse_rows),
        slice(TR + coarse_rows, TR + 2 * coarse_rows),
    )

    def pair_copy(k):
        return pltpu.make_async_remote_copy(
            src_ref=pair_send.at[k],
            dst_ref=pair_recv.at[k],
            send_sem=pair_ss.at[k],
            recv_sem=pair_rs.at[k],
            device_id=at(twin, c),
            device_id_type=MESH,
        )

    def to_twin(k, carry):
        line = lax.rem(z + 1 + k, pairs)
        for part, value in zip(pieces, row_pass(line * 2 + 1 - y)):
            pair_send[k, part, :] = value.astype(BF16)
        pair_copy(k).start()
        return carry

    lax.fori_loop(0, pairs, to_twin, 0)

    own_nodes = nodes_ref[...]
    after = nodes_beside[1:2, 0:1]
    is_last = c == lax.axis_size("mcol") - 1
    x_pan = col_coord(own_nodes, after, is_last, col_nodes, iota((1, TC), 1), 0.0)
    for k in range(KC):
        size = cols // KC
        pixel = (c * KC + k) * size + iota((size, TC), 0)
        col_weight[k * size : (k + 1) * size, :] = cubic_weight(
            x_pan - pixel.astype(F32)
        ).astype(BF16)
    x_ms = col_coord(own_nodes, after, is_last, col_nodes, 4 * iota((1, coarse_cols), 1) + 1, 0.5)
    x_ms = (x_ms - 1.5) * 0.25
    ms_col_weight[...] = jnp.zeros_like(ms_col_weight)
    for k in range(KC):
        pixel = (c * KC + k) * coarse_size + iota((coarse_size, coarse_cols), 0)
        weight = cubic_weight(x_ms - pixel.astype(F32)).astype(BF16)
        for b in range(bands):
            row = (k * bands + b) * coarse_size
            ms_col_weight[row : row + coarse_size, b * coarse_cols : (b + 1) * coarse_cols] = weight

    def owner_copy(k, line, slot):
        return pltpu.make_async_remote_copy(
            src_ref=owner_send.at[k],
            dst_ref=owner_recv.at[slot],
            send_sem=owner_ss.at[k],
            recv_sem=owner_rs.at[slot],
            device_id=at(line * 2 + y, c),
            device_id_type=MESH,
        )

    def to_owner(k, carry):
        line = lax.rem(z + 1 + k, pairs)
        values = row_pass(line * 2 + y)
        pair_copy(k).wait()
        for part, value in zip(pieces, values):
            owner_send[k, part, :] = (value + pair_recv[k, part, :].astype(F32)).astype(BF16)
        owner_copy(k, line, z).start()
        return carry

    lax.fori_loop(0, pairs - 1, to_owner, 0)
    values = row_pass(m)
    pair_copy(pairs - 1).wait()
    for part, value in zip(pieces, values):
        total[part, :] = value + pair_recv[pairs - 1, part, :].astype(F32)

    def from_line(k, carry):
        line = lax.rem(z + pairs - 1 - k, pairs)
        owner_copy(k, line, line).wait()
        total[...] += owner_recv[line].astype(F32)
        return carry

    lax.fori_loop(0, pairs - 1, from_line, 0)

    ms_sum = [total[part, :].astype(BF16) for part in pieces[1:]]
    ms_map = jnp.dot(ms_sum[0], ms_col_weight[0:cols, :], preferred_element_type=F32)
    ms_map = ms_map + jnp.dot(
        ms_sum[1], ms_col_weight[cols : 2 * cols, :], preferred_element_type=F32
    )
    window[half : half + coarse_rows, :] = ms_map.astype(BF16)

    has_above, has_below = m > 0, m < n - 1

    def halo_copy(k, src, dst, row, col):
        return pltpu.make_async_remote_copy(
            src_ref=window.at[pl.ds(src, half)] if k else window.at[pl.ds(src, coarse_rows)],
            dst_ref=dst,
            send_sem=halo_ss.at[k],
            recv_sem=halo_rs.at[k],
            device_id=at(row, col),
            device_id_type=MESH,
        )

    mid = half + coarse_rows
    across_copy = halo_copy(0, half, beside.at[pl.ds(half, coarse_rows)], m, other)
    up_copies = [
        halo_copy(1, half, window.at[pl.ds(mid, half)], m - 1, c),
        halo_copy(2, half, beside.at[pl.ds(mid, half)], m - 1, other),
    ]
    down_copies = [
        halo_copy(3, coarse_rows, window.at[pl.ds(0, half)], m + 1, c),
        halo_copy(4, coarse_rows, beside.at[pl.ds(0, half)], m + 1, other),
    ]
    across_copy.start()

    @pl.when(has_above)
    def _():
        for copy in up_copies:
            copy.start()

    @pl.when(has_below)
    def _():
        for copy in down_copies:
            copy.start()

    pan_map[...] = jnp.dot(
        total[pieces[0], :].astype(BF16), col_weight[...], preferred_element_type=F32
    )

    across_copy.wait()

    @pl.when(has_above)
    def _():
        for copy in up_copies:
            copy.wait_send()
        for copy in down_copies:
            copy.wait_recv()

    @pl.when(has_below)
    def _():
        for copy in down_copies:
            copy.wait_send()
        for copy in up_copies:
            copy.wait_recv()

    @pl.when(jnp.logical_not(has_above))
    def _():
        window[0:half, :] = jnp.zeros((half, window.shape[1]), BF16)
        beside[0:half, :] = jnp.zeros((half, window.shape[1]), BF16)

    @pl.when(jnp.logical_not(has_below))
    def _():
        window[mid : mid + half, :] = jnp.zeros((half, window.shape[1]), BF16)
        beside[mid : mid + half, :] = jnp.zeros((half, window.shape[1]), BF16)

    for b in range(bands):
        lanes = slice(b * coarse_cols, (b + 1) * coarse_cols)
        across = jnp.dot(window[:, lanes], up_cols[0], preferred_element_type=F32)
        across = across + jnp.dot(beside[:, lanes], up_cols[1], preferred_element_type=F32)
        upsampled[b] = jnp.dot(up_rows[...], across.astype(BF16), preferred_element_type=F32)

    def combine(k, carry):
        rows = pl.ds(pl.multiple_of(k * 16, 16), 16)
        for lane in range(0, TC, 128):
            values = [upsampled[b, rows, lane : lane + 128] for b in range(bands)]
            pan = pan_map[rows, lane : lane + 128]
            for b in range(bands):
                mixed = gain_ref[b] * pan
                for other_band in range(bands):
                    mixed = mixed + mix_ref[b, other_band] * values[other_band]
                out_ref[b, rows, lane : lane + 128] = mixed.astype(BF16)
        return carry

    lax.fori_loop(0, TR // 16, combine, 0)


def local(
    pan_blocks,
    ms_blocks,
    send_list,
    tile_list,
    row_grid,
    col_grid,
    band_mix,
    band_gain,
    synth_weight,
):
    n = lax.axis_size("mrow")
    pairs = n // 2
    own_blocks, block_size, _ = pan_blocks.shape
    _, coarse_size, coarse_width = ms_blocks.shape
    slots = tile_list.shape[1]
    capacity = slots // n
    bands = band_gain.shape[0]
    pan_rows, pan_cols = KR * block_size, KC * block_size
    ms_rows, ms_cols = KR * coarse_size, KC * coarse_width
    smem = pl.BlockSpec(memory_space=pltpu.SMEM)
    vmem = pl.BlockSpec(memory_space=pltpu.VMEM)
    pan_cells, ms_cells = pl.pallas_call(
        functools.partial(cell_sums, capacity),
        grid=(n,),
        out_shape=(
            jax.ShapeDtypeStruct((n, pan_rows, pan_cols), BF16),
            jax.ShapeDtypeStruct((n, ms_rows, ms_cols), BF16),
        ),
        in_specs=[smem, vmem, vmem],
        out_specs=(
            pl.BlockSpec((1, pan_rows, pan_cols), lambda t: (t, 0, 0)),
            pl.BlockSpec((1, ms_rows, ms_cols), lambda t: (t, 0, 0)),
        ),
        scratch_shapes=[
            pltpu.SMEM((slots,), jnp.int32),
            pltpu.VMEM((pan_rows, pan_cols), F32),
            pltpu.VMEM((ms_rows, ms_cols), F32),
        ],
        name="cell_sums",
    )(send_list, pan_blocks, ms_blocks)

    nodes = jnp.concatenate(
        [
            jnp.pad(row_grid[None, :], ((0, 0), (0, 128 - row_grid.shape[0]))),
            jnp.pad(col_grid, ((0, 6), (0, 128 - col_grid.shape[1]))),
        ],
        axis=0,
    )
    mix = jnp.eye(bands, dtype=F32) + band_mix - band_gain[:, None] * synth_weight[None, :]
    coarse_rows, coarse_cols = TR // 4, TC // 4
    piece_rows = TR + 2 * coarse_rows
    dma = pltpu.SemaphoreType.DMA
    return pl.pallas_call(
        functools.partial(mapping, col_grid.shape[1]),
        out_shape=jax.ShapeDtypeStruct((bands, TR, TC), BF16),
        in_specs=[vmem, vmem, vmem, smem, smem],
        out_specs=vmem,
        scratch_shapes=[
            pltpu.VMEM((n, 8, 128), F32),
            pltpu.VMEM((8, 128), F32),
            pltpu.VMEM((pairs, piece_rows, pan_cols), BF16),
            pltpu.VMEM((pairs, piece_rows, pan_cols), BF16),
            pltpu.VMEM((pairs, piece_rows, pan_cols), BF16),
            pltpu.VMEM((pairs, piece_rows, pan_cols), BF16),
            pltpu.VMEM((piece_rows, pan_cols), F32),
            pltpu.VMEM((pan_cols, TC), BF16),
            pltpu.VMEM((ms_cols, bands * coarse_cols), BF16),
            pltpu.VMEM((2 * coarse_rows, bands * coarse_cols), BF16),
            pltpu.VMEM((2 * coarse_rows, bands * coarse_cols), BF16),
            pltpu.VMEM((2, coarse_cols, TC), BF16),
            pltpu.VMEM((TR, 2 * coarse_rows), BF16),
            pltpu.VMEM((TR, TC), F32),
            pltpu.VMEM((bands, TR, TC), F32),
            dma((n + 1,)),
            dma((n + 1,)),
            dma((pairs,)),
            dma((pairs,)),
            dma((pairs,)),
            dma((pairs,)),
            dma((5,)),
            dma((5,)),
        ],
        compiler_params=pltpu.CompilerParams(
            collective_id=0, has_side_effects=True, vmem_limit_bytes=60 * 1024 * 1024
        ),
        name="mapping",
    )(nodes, pan_cells, ms_cells, mix, band_gain)


def solution(mesh):
    return jax.shard_map(
        local,
        mesh=mesh,
        in_specs=(
            P(("scene", "mrow", "mcol"), None, None),
            P(("scene", "mrow", "mcol"), None, None),
            P(None, ("scene", "mrow", "mcol")),
            P(None, ("scene", "mrow", "mcol")),
            P(("scene", "mrow")),
            P(("scene", "mrow"), "mcol"),
            P(),
            P(),
            P(),
        ),
        out_specs=P(None, ("scene", "mrow"), "mcol"),
        check_vma=False,
    )
```

```python
import functools

import jax
import jax.numpy as jnp
from jax import lax
from jax.experimental import pallas as pl
from jax.experimental.pallas import tpu as pltpu
from jax.sharding import PartitionSpec as P

GRID = 64
TR = 128
TC = 512
KR = 2
KC = 5
MESH = pl.DeviceIdType.MESH
F32 = jnp.float32
BF16 = jnp.bfloat16


def cubic_weight(offset):
    outer = jnp.maximum(2.0 - jnp.abs(offset), 0.0)
    shifted = outer - 1.0
    inner = jnp.maximum(shifted, 0.0)
    return outer * outer * (0.5 * shifted) + inner * inner * (1.0 - 2.0 * inner)


def iota(shape, dim):
    return lax.broadcasted_iota(jnp.int32, shape, dim)


def cell_sums(
    capacity,
    send_ref,
    pan_ref,
    ms_ref,
    row_ref,
    col_ref,
    pan_out,
    ms_out,
    nodes_out,
    slot_block,
    pan_acc,
    ms_acc,
):
    tile = pl.program_id(0)
    own_blocks, block_size, _ = pan_ref.shape
    _, coarse_size, coarse_width = ms_ref.shape
    first_col = lax.axis_index("mcol") * KC

    @pl.when(tile == 0)
    def _():
        nodes_out[...] = jnp.zeros_like(nodes_out)
        nodes_out[0:1, 0 : row_ref.shape[1]] = row_ref[...]
        nodes_out[1:2, 0 : col_ref.shape[1]] = col_ref[...]

        def clear(slot, carry):
            slot_block[slot] = -1
            return carry

        lax.fori_loop(0, slot_block.shape[0], clear, 0)

        def enter(block, carry):
            slot_block[send_ref[0, block]] = block
            return carry

        lax.fori_loop(0, own_blocks, enter, 0)

    pan_acc[...] = jnp.zeros_like(pan_acc)
    ms_acc[...] = jnp.zeros_like(ms_acc)

    def add(slot, carry):
        block = slot_block[tile * capacity + slot]

        @pl.when(block >= 0)
        def _():
            row = send_ref[1, block]
            col = send_ref[2, block] - first_col
            at = (
                pl.ds(pl.multiple_of(row * block_size, block_size), block_size),
                pl.ds(pl.multiple_of(col * block_size, block_size), block_size),
            )
            pan_acc[at] += pan_ref[block].astype(F32)
            at = (
                pl.ds(pl.multiple_of(row * coarse_size, coarse_size), coarse_size),
                pl.ds(pl.multiple_of(col * coarse_width, coarse_width), coarse_width),
            )
            ms_acc[at] += ms_ref[block].astype(F32)

        return carry

    lax.fori_loop(0, capacity, add, 0)
    pan_out[0] = pan_acc[...].astype(BF16)
    ms_out[0] = ms_acc[...].astype(BF16)


def row_coord(nodes, position, offset):
    first = position < GRID
    a = jnp.where(first, nodes[0:1, 0:1], nodes[0:1, 1:2])
    b = jnp.where(first, nodes[0:1, 1:2], nodes[0:1, 2:3])
    within = (jnp.where(first, position, position - GRID).astype(F32) + offset) / GRID
    return a + (b - a) * within


def col_coord(nodes, after, is_last, count, position, offset):
    segment = position // GRID
    coord = jnp.zeros(position.shape, F32)
    for s in range(count):
        left, shift = nodes[1:2, s : s + 1], s * GRID
        if s + 1 < count:
            right = nodes[1:2, s + 1 : s + 2]
        else:
            right = jnp.where(is_last, left, after)
            left = jnp.where(is_last, nodes[1:2, s - 1 : s], left)
            shift = jnp.where(is_last, shift - GRID, shift)
        within = ((position - shift).astype(F32) + offset) / GRID
        coord = jnp.where(segment == s, left + (right - left) * within, coord)
    return coord


def mapping(
    col_nodes,
    nodes_ref,
    pan_hbm,
    ms_hbm,
    mix_ref,
    gain_ref,
    synth_ref,
    mixed_hbm,
    pan_map,
    pan_ref,
    ms_ref,
    nodes_all,
    ms_pair_send,
    ms_pair_recv,
    ms_owner_send,
    ms_owner_recv,
    pan_pair_send,
    pan_pair_recv,
    pan_owner_send,
    pan_owner_recv,
    ms_total,
    col_weight,
    ms_col_weight,
    window,
    beside,
    up_cols,
    up_rows,
    upsampled,
    mixed,
    load_sem,
    nodes_ss,
    nodes_rs,
    ms_pair_ss,
    ms_pair_rs,
    ms_owner_ss,
    ms_owner_rs,
    pan_pair_ss,
    pan_pair_rs,
    pan_owner_ss,
    pan_owner_rs,
    halo_ss,
    halo_rs,
):
    n = lax.axis_size("mrow")
    pairs = n // 2
    scene = lax.axis_index("scene")
    m = lax.axis_index("mrow")
    c = lax.axis_index("mcol")
    z, y = m // 2, m % 2
    twin = z * 2 + (1 - y)
    other = 1 - c
    cols = pan_ref.shape[2]
    pan_rows = pan_ref.shape[1]
    ms_rows = ms_ref.shape[1]
    bands = mixed.shape[0]
    coarse_rows = TR // 4
    coarse_cols = TC // 4
    half = coarse_rows // 2
    mid = half + coarse_rows
    coarse_size = ms_rows // KR
    is_last = c == lax.axis_size("mcol") - 1

    def at(row, col):
        return (scene, row, col)

    def line_of(k):
        return lax.rem(z + 1 + lax.rem(pairs // 2 - 1 + k, pairs - 1), pairs)

    barrier = pltpu.get_barrier_semaphore()

    def greet(k, carry):
        row = lax.rem(m + k, n)
        pl.semaphore_signal(barrier, inc=1, device_id=at(row, c), device_id_type=MESH)
        pl.semaphore_signal(barrier, inc=1, device_id=at(row, other), device_id_type=MESH)
        return carry

    pl.semaphore_signal(barrier, inc=1, device_id=at(m, other), device_id_type=MESH)
    lax.fori_loop(1, n, greet, 0)
    ms_load = pltpu.make_async_copy(ms_hbm, ms_ref, load_sem.at[0])
    pan_load = pltpu.make_async_copy(pan_hbm, pan_ref, load_sem.at[1])
    ms_load.start()
    pan_load.start()

    tap = iota((TR, 2 * coarse_rows), 1) - (half - 2)
    spot = (iota((TR, 2 * coarse_rows), 0).astype(F32) - 1.5) * 0.25 + 2.0
    up_rows[...] = cubic_weight(spot - tap.astype(F32)).astype(BF16)
    ms_col_weight[...] = jnp.zeros_like(ms_col_weight)
    pl.semaphore_wait(barrier, 2 * n - 1)

    def nodes_copy(slot_row, slot_col, row, col):
        return pltpu.make_async_remote_copy(
            src_ref=nodes_ref,
            dst_ref=nodes_all.at[slot_col, slot_row],
            send_sem=nodes_ss.at[col, row],
            recv_sem=nodes_rs.at[slot_col, slot_row],
            device_id=at(row, col),
            device_id_type=MESH,
        )

    def send_nodes(k, carry):
        row = lax.rem(m + k, n)
        nodes_copy(m, c, row, c).start()
        nodes_copy(m, c, row, other).start()
        return carry

    lax.fori_loop(1, n, send_nodes, 0)
    nodes_copy(m, c, m, other).start()
    nodes_all[c, m] = nodes_ref[...]

    spot = (iota((coarse_cols, TC), 1).astype(F32) - 1.5) * 0.25 + 2.0
    tap = iota((coarse_cols, TC), 0) + 2
    up_cols[0] = cubic_weight(spot - tap.astype(F32)).astype(BF16)
    tap = tap + jnp.where(c == 0, coarse_cols, -coarse_cols)
    up_cols[1] = cubic_weight(spot - tap.astype(F32)).astype(BF16)
    ms_load.wait()

    def wait_nodes(k, carry):
        row = lax.rem(m + k, n)
        nodes_copy(row, c, row, c).wait()
        nodes_copy(row, other, row, other).wait()
        return carry

    lax.fori_loop(1, n, wait_nodes, 0)
    nodes_copy(m, other, m, other).wait()

    sides = (slice(0, coarse_rows), slice(coarse_rows, 2 * coarse_rows))

    def ms_part(tile):
        nodes = nodes_all[c, tile]
        shape = (coarse_rows, ms_rows)
        spots = (row_coord(nodes, 4 * iota(shape, 0) + 1, 0.5) - 1.5) * 0.25
        weight = cubic_weight(spots - iota(shape, 1).astype(F32)).astype(BF16)
        left = jnp.dot(weight, ms_ref[tile, :, 0:cols], preferred_element_type=F32)
        right = jnp.dot(weight, ms_ref[tile, :, cols : 2 * cols], preferred_element_type=F32)
        return left, right

    def pan_part(tile):
        nodes = nodes_all[c, tile]
        after = nodes_all[1, tile][1:2, 0:1]
        x_pan = col_coord(nodes, after, is_last, col_nodes, iota((1, TC), 1), 0.0)
        size = cols // KC
        for k in range(KC):
            pixel = (c * KC + k) * size + iota((size, TC), 0)
            col_weight[k * size : (k + 1) * size, :] = cubic_weight(
                x_pan - pixel.astype(F32)
            ).astype(BF16)
        shape = (TR, pan_rows)
        weight = cubic_weight(
            row_coord(nodes, iota(shape, 0), 0.0) - iota(shape, 1).astype(F32)
        ).astype(BF16)
        rows = jnp.dot(weight, pan_ref[tile], preferred_element_type=F32)
        return jnp.dot(rows.astype(BF16), col_weight[...], preferred_element_type=F32)

    def pair_copy(send, recv, ss, rs, k):
        return pltpu.make_async_remote_copy(
            src_ref=send.at[k],
            dst_ref=recv.at[k],
            send_sem=ss.at[k],
            recv_sem=rs.at[k],
            device_id=at(twin, c),
            device_id_type=MESH,
        )

    def owner_copy(send, recv, ss, rs, k, line, slot):
        return pltpu.make_async_remote_copy(
            src_ref=send.at[k],
            dst_ref=recv.at[slot],
            send_sem=ss.at[k],
            recv_sem=rs.at[slot],
            device_id=at(line * 2 + y, c),
            device_id_type=MESH,
        )

    ms_pair = functools.partial(pair_copy, ms_pair_send, ms_pair_recv, ms_pair_ss, ms_pair_rs)
    pan_pair = functools.partial(pair_copy, pan_pair_send, pan_pair_recv, pan_pair_ss, pan_pair_rs)
    ms_owner = functools.partial(
        owner_copy, ms_owner_send, ms_owner_recv, ms_owner_ss, ms_owner_rs
    )
    pan_owner = functools.partial(
        owner_copy, pan_owner_send, pan_owner_recv, pan_owner_ss, pan_owner_rs
    )

    def ms_to_twin(k, tile):
        for side, value in zip(sides, ms_part(tile)):
            ms_pair_send[k, side, :] = value.astype(BF16)
        ms_pair(k).start()

    def pan_to_twin(k, tile):
        pan_pair_send[k] = pan_part(tile).astype(BF16)
        pan_pair(k).start()

    def each_line(first, last, step):
        def body(k, carry):
            step(k, line_of(k))
            return carry

        lax.fori_loop(first, last, body, 0)

    each_line(0, pairs - 1, lambda k, line: ms_to_twin(k, line * 2 + 1 - y))
    ms_to_twin(pairs - 1, twin)
    pan_load.wait()
    each_line(0, pairs - 1, lambda k, line: pan_to_twin(k, line * 2 + 1 - y))
    pan_to_twin(pairs - 1, twin)

    def ms_to_owner(k, line):
        values = ms_part(line * 2 + y)
        ms_pair(k).wait()
        for side, value in zip(sides, values):
            ms_owner_send[k, side, :] = (value + ms_pair_recv[k, side, :].astype(F32)).astype(BF16)
        ms_owner(k, line, z).start()

    each_line(0, pairs - 1, ms_to_owner)
    values = ms_part(m)
    ms_pair(pairs - 1).wait()
    for side, value in zip(sides, values):
        ms_total[side, :] = value + ms_pair_recv[pairs - 1, side, :].astype(F32)

    x_ms = col_coord(
        nodes_ref[...],
        nodes_all[1, m][1:2, 0:1],
        is_last,
        col_nodes,
        4 * iota((1, coarse_cols), 1) + 1,
        0.5,
    )
    x_ms = (x_ms - 1.5) * 0.25
    for k in range(KC):
        pixel = (c * KC + k) * coarse_size + iota((coarse_size, coarse_cols), 0)
        weight = cubic_weight(x_ms - pixel.astype(F32)).astype(BF16)
        for b in range(bands):
            row = (k * bands + b) * coarse_size
            ms_col_weight[row : row + coarse_size, b * coarse_cols : (b + 1) * coarse_cols] = weight

    def pan_to_owner(k, line):
        value = pan_part(line * 2 + y)
        pan_pair(k).wait()
        pan_owner_send[k] = (value + pan_pair_recv[k].astype(F32)).astype(BF16)
        pan_owner(k, line, z).start()

    each_line(0, pairs - 2, pan_to_owner)

    def ms_from_line(k, line):
        ms_owner(k, line, line).wait()
        ms_total[...] += ms_owner_recv[line].astype(F32)

    each_line(0, pairs - 1, ms_from_line)
    left, right = [ms_total[side, :].astype(BF16) for side in sides]
    ms_map = jnp.dot(left, ms_col_weight[0:cols, :], preferred_element_type=F32)
    ms_map = ms_map + jnp.dot(
        right, ms_col_weight[cols : 2 * cols, :], preferred_element_type=F32
    )
    window[half:mid, :] = ms_map.astype(BF16)

    has_above, has_below = m > 0, m < n - 1

    def halo_copy(k, src, rows, dst, start, row, col):
        return pltpu.make_async_remote_copy(
            src_ref=window.at[pl.ds(src, rows)],
            dst_ref=dst.at[pl.ds(start, rows)],
            send_sem=halo_ss.at[k],
            recv_sem=halo_rs.at[k],
            device_id=at(row, col),
            device_id_type=MESH,
        )

    across_copy = halo_copy(0, half, coarse_rows, beside, half, m, other)
    up_copies = [
        halo_copy(1, half, half, window, mid, m - 1, c),
        halo_copy(2, half, half, beside, mid, m - 1, other),
    ]
    down_copies = [
        halo_copy(3, coarse_rows, half, window, 0, m + 1, c),
        halo_copy(4, coarse_rows, half, beside, 0, m + 1, other),
    ]
    across_copy.start()

    @pl.when(has_above)
    def _():
        for copy in up_copies:
            copy.start()

    @pl.when(has_below)
    def _():
        for copy in down_copies:
            copy.start()

    pan_to_owner(pairs - 2, line_of(pairs - 2))
    pan_map[...] = pan_part(m)
    across_copy.wait()

    @pl.when(has_above)
    def _():
        for copy in up_copies:
            copy.wait_send()
        for copy in down_copies:
            copy.wait_recv()

    @pl.when(has_below)
    def _():
        for copy in down_copies:
            copy.wait_send()
        for copy in up_copies:
            copy.wait_recv()

    edge = jnp.zeros((half, window.shape[1]), BF16)

    @pl.when(jnp.logical_not(has_above))
    def _():
        window[0:half, :] = edge
        beside[0:half, :] = edge

    @pl.when(jnp.logical_not(has_below))
    def _():
        window[mid : mid + half, :] = edge
        beside[mid : mid + half, :] = edge

    for b in range(bands):
        lanes = slice(b * coarse_cols, (b + 1) * coarse_cols)
        across = jnp.dot(window[:, lanes], up_cols[0], preferred_element_type=F32)
        across = across + jnp.dot(beside[:, lanes], up_cols[1], preferred_element_type=F32)
        upsampled[b] = jnp.dot(up_rows[...], across.astype(BF16), preferred_element_type=F32)

    def mix_bands(k, carry):
        rows = pl.ds(pl.multiple_of(k * 16, 16), 16)
        for lane in range(0, TC, 128):
            values = [upsampled[b, rows, lane : lane + 128] for b in range(bands)]
            synthetic = sum(synth_ref[b] * values[b] for b in range(bands))
            for b in range(bands):
                result = values[b] - gain_ref[b] * synthetic
                for k2 in range(bands):
                    result = result + mix_ref[b, k2] * values[k2]
                mixed[b, rows, lane : lane + 128] = result.astype(BF16)
        return carry

    lax.fori_loop(0, TR // 16, mix_bands, 0)
    store = pltpu.make_async_copy(mixed, mixed_hbm, load_sem.at[2])
    store.start()

    pan_pair(pairs - 1).wait()
    pan_map[...] += pan_pair_recv[pairs - 1].astype(F32)

    def pan_from_line(k, line):
        pan_owner(k, line, line).wait()
        pan_map[...] += pan_owner_recv[line].astype(F32)

    each_line(0, pairs - 1, pan_from_line)
    store.wait()


def local(
    pan_blocks,
    ms_blocks,
    send_list,
    tile_list,
    row_grid,
    col_grid,
    band_mix,
    band_gain,
    synth_weight,
):
    n = lax.axis_size("mrow")
    pairs = n // 2
    own_blocks, block_size, _ = pan_blocks.shape
    _, coarse_size, coarse_width = ms_blocks.shape
    slots = tile_list.shape[1]
    capacity = slots // n
    bands = band_gain.shape[0]
    pan_rows, pan_cols = KR * block_size, KC * block_size
    ms_rows, ms_cols = KR * coarse_size, KC * coarse_width
    smem = pl.BlockSpec(memory_space=pltpu.SMEM)
    vmem = pl.BlockSpec(memory_space=pltpu.VMEM)
    hbm = pl.BlockSpec(memory_space=pl.ANY)
    pan_cells, ms_cells, nodes = pl.pallas_call(
        functools.partial(cell_sums, capacity),
        grid=(n,),
        out_shape=(
            jax.ShapeDtypeStruct((n, pan_rows, pan_cols), BF16),
            jax.ShapeDtypeStruct((n, ms_rows, ms_cols), BF16),
            jax.ShapeDtypeStruct((8, 128), F32),
        ),
        in_specs=[smem, vmem, vmem, vmem, vmem],
        out_specs=(
            pl.BlockSpec((1, pan_rows, pan_cols), lambda t: (t, 0, 0)),
            pl.BlockSpec((1, ms_rows, ms_cols), lambda t: (t, 0, 0)),
            pl.BlockSpec((8, 128), lambda t: (0, 0)),
        ),
        scratch_shapes=[
            pltpu.SMEM((slots,), jnp.int32),
            pltpu.VMEM((pan_rows, pan_cols), F32),
            pltpu.VMEM((ms_rows, ms_cols), F32),
        ],
        name="cell_sums",
    )(send_list, pan_blocks, ms_blocks, row_grid[None, :], col_grid)

    coarse_rows, coarse_cols = TR // 4, TC // 4
    dma = pltpu.SemaphoreType.DMA
    ms_slots = pltpu.VMEM((pairs, 2 * coarse_rows, pan_cols), BF16)
    pan_slots = pltpu.VMEM((pairs, TR, TC), BF16)
    mixed, pan_map = pl.pallas_call(
        functools.partial(mapping, col_grid.shape[1]),
        out_shape=(
            jax.ShapeDtypeStruct((bands, TR, TC), BF16),
            jax.ShapeDtypeStruct((TR, TC), F32),
        ),
        in_specs=[vmem, hbm, hbm, smem, smem, smem],
        out_specs=(hbm, vmem),
        scratch_shapes=[
            pltpu.VMEM((n, pan_rows, pan_cols), BF16),
            pltpu.VMEM((n, ms_rows, ms_cols), BF16),
            pltpu.VMEM((2, n, 8, 128), F32),
            ms_slots,
            ms_slots,
            ms_slots,
            ms_slots,
            pan_slots,
            pan_slots,
            pan_slots,
            pan_slots,
            pltpu.VMEM((2 * coarse_rows, pan_cols), F32),
            pltpu.VMEM((pan_cols, TC), BF16),
            pltpu.VMEM((ms_cols, bands * coarse_cols), BF16),
            pltpu.VMEM((2 * coarse_rows, bands * coarse_cols), BF16),
            pltpu.VMEM((2 * coarse_rows, bands * coarse_cols), BF16),
            pltpu.VMEM((2, coarse_cols, TC), BF16),
            pltpu.VMEM((TR, 2 * coarse_rows), BF16),
            pltpu.VMEM((bands, TR, TC), F32),
            pltpu.VMEM((bands, TR, TC), BF16),
            dma((3,)),
            dma((2, n)),
            dma((2, n)),
        ]
        + [dma((pairs,))] * 8
        + [dma((5,)), dma((5,))],
        compiler_params=pltpu.CompilerParams(
            collective_id=0, has_side_effects=True, vmem_limit_bytes=60 * 1024 * 1024
        ),
        name="mapping",
    )(nodes, pan_cells, ms_cells, band_mix, band_gain, synth_weight)
    detail = band_gain[:, None, None] * pan_map[None]
    return (mixed.astype(F32) + detail).astype(BF16)


def solution(mesh):
    return jax.shard_map(
        local,
        mesh=mesh,
        in_specs=(
            P(("scene", "mrow", "mcol"), None, None),
            P(("scene", "mrow", "mcol"), None, None),
            P(None, ("scene", "mrow", "mcol")),
            P(None, ("scene", "mrow", "mcol")),
            P(("scene", "mrow")),
            P(("scene", "mrow"), "mcol"),
            P(),
            P(),
            P(),
        ),
        out_specs=P(None, ("scene", "mrow"), "mcol"),
        check_vma=False,
    )
```

```python
import functools

import jax
import jax.numpy as jnp
from jax import lax
from jax.experimental import pallas as pl
from jax.experimental.pallas import tpu as pltpu
from jax.sharding import PartitionSpec as P

GRID = 64
TR = 128
TC = 512
KR = 2
KC = 5
MESH = pl.DeviceIdType.MESH
F32 = jnp.float32
BF16 = jnp.bfloat16


def cubic_weight(offset):
    outer = jnp.maximum(2.0 - jnp.abs(offset), 0.0)
    shifted = outer - 1.0
    inner = jnp.maximum(shifted, 0.0)
    return outer * outer * (0.5 * shifted) + inner * inner * (1.0 - 2.0 * inner)


def iota(shape, dim):
    return lax.broadcasted_iota(jnp.int32, shape, dim)


def cell_sums(
    capacity,
    send_ref,
    pan_ref,
    ms_ref,
    row_ref,
    col_ref,
    pan_out,
    ms_out,
    nodes_out,
    first_block,
    next_block,
):
    tile = pl.program_id(0)
    own_blocks, block_size, _ = pan_ref.shape
    _, coarse_size, coarse_width = ms_ref.shape
    first_col = lax.axis_index("mcol") * KC

    @pl.when(tile == 0)
    def _():
        nodes_out[...] = jnp.zeros_like(nodes_out)
        nodes_out[0:1, 0 : row_ref.shape[1]] = row_ref[...]
        nodes_out[1:2, 0 : col_ref.shape[1]] = col_ref[...]

        def clear(k, carry):
            for r in range(KR * KC):
                first_block[k * (KR * KC) + r] = -1
            return carry

        lax.fori_loop(0, first_block.shape[0] // (KR * KC), clear, 0)

        def enter(block, carry):
            cell = (send_ref[0, block] // capacity * KR + send_ref[1, block]) * KC
            cell = cell + send_ref[2, block] - first_col
            next_block[block] = first_block[cell]
            first_block[cell] = block
            return carry

        lax.fori_loop(0, own_blocks, enter, 0, unroll=4)

    for row in range(KR):
        for col in range(KC):

            def add(carry):
                block, pan, ms = carry
                pan = pan + pan_ref[block].astype(F32)
                ms = ms + ms_ref[block].astype(F32)
                return next_block[block], pan, ms

            start = (
                first_block[(tile * KR + row) * KC + col],
                jnp.zeros((block_size, block_size), F32),
                jnp.zeros((coarse_size, coarse_width), F32),
            )
            _, pan, ms = lax.while_loop(lambda carry: carry[0] >= 0, add, start)
            rows = slice(row * block_size, (row + 1) * block_size)
            pan_out[0, rows, col * block_size : (col + 1) * block_size] = pan.astype(BF16)
            rows = slice(row * coarse_size, (row + 1) * coarse_size)
            ms_out[0, rows, col * coarse_width : (col + 1) * coarse_width] = ms.astype(BF16)


def row_coord(nodes, position, offset):
    first = position < GRID
    a = jnp.where(first, nodes[0:1, 0:1], nodes[0:1, 1:2])
    b = jnp.where(first, nodes[0:1, 1:2], nodes[0:1, 2:3])
    within = (jnp.where(first, position, position - GRID).astype(F32) + offset) / GRID
    return a + (b - a) * within


def col_coord(nodes, after, is_last, count, position, offset):
    segment = position // GRID
    coord = jnp.zeros(position.shape, F32)
    for s in range(count):
        left, shift = nodes[1:2, s : s + 1], s * GRID
        if s + 1 < count:
            right = nodes[1:2, s + 1 : s + 2]
        else:
            right = jnp.where(is_last, left, after)
            left = jnp.where(is_last, nodes[1:2, s - 1 : s], left)
            shift = jnp.where(is_last, shift - GRID, shift)
        within = ((position - shift).astype(F32) + offset) / GRID
        coord = jnp.where(segment == s, left + (right - left) * within, coord)
    return coord


def mapping(
    col_nodes,
    nodes_ref,
    pan_hbm,
    ms_hbm,
    mix_ref,
    gain_ref,
    synth_ref,
    mixed_hbm,
    pan_map,
    pan_ref,
    ms_ref,
    nodes_all,
    ms_pair_send,
    ms_pair_recv,
    ms_owner_send,
    ms_owner_recv,
    pan_pair_send,
    pan_pair_recv,
    pan_owner_send,
    pan_owner_recv,
    ms_total,
    col_weight,
    ms_col_weight,
    window,
    beside,
    up_cols,
    up_rows,
    mixed,
    load_sem,
    nodes_ss,
    nodes_rs,
    ms_pair_ss,
    ms_pair_rs,
    ms_owner_ss,
    ms_owner_rs,
    pan_pair_ss,
    pan_pair_rs,
    pan_owner_ss,
    pan_owner_rs,
    halo_ss,
    halo_rs,
):
    n = lax.axis_size("mrow")
    pairs = n // 2
    scene = lax.axis_index("scene")
    m = lax.axis_index("mrow")
    c = lax.axis_index("mcol")
    z, y = m // 2, m % 2
    twin = z * 2 + (1 - y)
    other = 1 - c
    cols = pan_ref.shape[2]
    pan_rows = pan_ref.shape[1]
    ms_rows = ms_ref.shape[1]
    bands = mixed.shape[0]
    coarse_rows = TR // 4
    coarse_cols = TC // 4
    half = coarse_rows // 2
    mid = half + coarse_rows
    coarse_size = ms_rows // KR
    is_last = c == lax.axis_size("mcol") - 1

    def at(row, col):
        return (scene, row, col)

    def line_of(k):
        return lax.rem(z + 1 + lax.rem(pairs // 2 - 1 + k, pairs - 1), pairs)

    barrier = pltpu.get_barrier_semaphore()

    def greet(k, carry):
        row = lax.rem(m + k, n)
        pl.semaphore_signal(barrier, inc=1, device_id=at(row, c), device_id_type=MESH)
        pl.semaphore_signal(barrier, inc=1, device_id=at(row, other), device_id_type=MESH)
        return carry

    pl.semaphore_signal(barrier, inc=1, device_id=at(m, other), device_id_type=MESH)
    lax.fori_loop(1, n, greet, 0)
    ms_load = pltpu.make_async_copy(ms_hbm, ms_ref, load_sem.at[0])
    pan_load = pltpu.make_async_copy(pan_hbm, pan_ref, load_sem.at[1])
    ms_load.start()
    pan_load.start()

    tap = iota((TR, 2 * coarse_rows), 1) - (half - 2)
    spot = (iota((TR, 2 * coarse_rows), 0).astype(F32) - 1.5) * 0.25 + 2.0
    up_rows[...] = cubic_weight(spot - tap.astype(F32)).astype(BF16)
    ms_col_weight[...] = jnp.zeros_like(ms_col_weight)
    pl.semaphore_wait(barrier, 2 * n - 1)

    def nodes_copy(slot_row, slot_col, row, col):
        return pltpu.make_async_remote_copy(
            src_ref=nodes_ref,
            dst_ref=nodes_all.at[slot_col, slot_row],
            send_sem=nodes_ss.at[col, row],
            recv_sem=nodes_rs.at[slot_col, slot_row],
            device_id=at(row, col),
            device_id_type=MESH,
        )

    def send_nodes(k, carry):
        row = lax.rem(m + k, n)
        nodes_copy(m, c, row, c).start()
        nodes_copy(m, c, row, other).start()
        return carry

    lax.fori_loop(1, n, send_nodes, 0)
    nodes_copy(m, c, m, other).start()
    nodes_all[c, m] = nodes_ref[...]

    spot = (iota((coarse_cols, TC), 1).astype(F32) - 1.5) * 0.25 + 2.0
    tap = iota((coarse_cols, TC), 0) + 2
    up_cols[0] = cubic_weight(spot - tap.astype(F32)).astype(BF16)
    tap = tap + jnp.where(c == 0, coarse_cols, -coarse_cols)
    up_cols[1] = cubic_weight(spot - tap.astype(F32)).astype(BF16)
    ms_load.wait()

    def wait_nodes(k, carry):
        row = lax.rem(m + k, n)
        nodes_copy(row, c, row, c).wait()
        nodes_copy(row, other, row, other).wait()
        return carry

    lax.fori_loop(1, n, wait_nodes, 0)
    nodes_copy(m, other, m, other).wait()

    sides = (slice(0, coarse_rows), slice(coarse_rows, 2 * coarse_rows))

    def ms_part(tile):
        nodes = nodes_all[c, tile]
        shape = (coarse_rows, ms_rows)
        spots = (row_coord(nodes, 4 * iota(shape, 0) + 1, 0.5) - 1.5) * 0.25
        weight = cubic_weight(spots - iota(shape, 1).astype(F32)).astype(BF16)
        left = jnp.dot(weight, ms_ref[tile, :, 0:cols], preferred_element_type=F32)
        right = jnp.dot(weight, ms_ref[tile, :, cols : 2 * cols], preferred_element_type=F32)
        return left, right

    def pan_part(tile):
        nodes = nodes_all[c, tile]
        after = nodes_all[1, tile][1:2, 0:1]
        x_pan = col_coord(nodes, after, is_last, col_nodes, iota((1, TC), 1), 0.0)
        size = cols // KC
        for k in range(KC):
            pixel = (c * KC + k) * size + iota((size, TC), 0)
            col_weight[k * size : (k + 1) * size, :] = cubic_weight(
                x_pan - pixel.astype(F32)
            ).astype(BF16)
        shape = (TR, pan_rows)
        weight = cubic_weight(
            row_coord(nodes, iota(shape, 0), 0.0) - iota(shape, 1).astype(F32)
        ).astype(BF16)
        rows = jnp.dot(weight, pan_ref[tile], preferred_element_type=F32)
        return jnp.dot(rows.astype(BF16), col_weight[...], preferred_element_type=F32)

    def pair_copy(send, recv, ss, rs, k):
        return pltpu.make_async_remote_copy(
            src_ref=send.at[k],
            dst_ref=recv.at[k],
            send_sem=ss.at[k],
            recv_sem=rs.at[k],
            device_id=at(twin, c),
            device_id_type=MESH,
        )

    def owner_copy(send, recv, ss, rs, k, line, slot):
        return pltpu.make_async_remote_copy(
            src_ref=send.at[k],
            dst_ref=recv.at[slot],
            send_sem=ss.at[k],
            recv_sem=rs.at[slot],
            device_id=at(line * 2 + y, c),
            device_id_type=MESH,
        )

    ms_pair = functools.partial(pair_copy, ms_pair_send, ms_pair_recv, ms_pair_ss, ms_pair_rs)
    pan_pair = functools.partial(pair_copy, pan_pair_send, pan_pair_recv, pan_pair_ss, pan_pair_rs)
    ms_owner = functools.partial(
        owner_copy, ms_owner_send, ms_owner_recv, ms_owner_ss, ms_owner_rs
    )
    pan_owner = functools.partial(
        owner_copy, pan_owner_send, pan_owner_recv, pan_owner_ss, pan_owner_rs
    )

    def ms_to_twin(k, tile):
        for side, value in zip(sides, ms_part(tile)):
            ms_pair_send[k, side, :] = value.astype(BF16)
        ms_pair(k).start()

    def pan_to_twin(k, tile):
        pan_pair_send[k] = pan_part(tile).astype(BF16)
        pan_pair(k).start()

    def each_line(first, last, step):
        def body(k, carry):
            step(k, line_of(k))
            return carry

        lax.fori_loop(first, last, body, 0)

    each_line(0, pairs - 1, lambda k, line: ms_to_twin(k, line * 2 + 1 - y))
    ms_to_twin(pairs - 1, twin)
    pan_load.wait()
    each_line(0, pairs - 1, lambda k, line: pan_to_twin(k, line * 2 + 1 - y))
    pan_to_twin(pairs - 1, twin)

    def ms_to_owner(k, line):
        values = ms_part(line * 2 + y)
        ms_pair(k).wait()
        for side, value in zip(sides, values):
            ms_owner_send[k, side, :] = (value + ms_pair_recv[k, side, :].astype(F32)).astype(BF16)
        ms_owner(k, line, z).start()

    each_line(0, pairs - 1, ms_to_owner)
    values = ms_part(m)
    ms_pair(pairs - 1).wait()
    for side, value in zip(sides, values):
        ms_total[side, :] = value + ms_pair_recv[pairs - 1, side, :].astype(F32)

    x_ms = col_coord(
        nodes_ref[...],
        nodes_all[1, m][1:2, 0:1],
        is_last,
        col_nodes,
        4 * iota((1, coarse_cols), 1) + 1,
        0.5,
    )
    x_ms = (x_ms - 1.5) * 0.25
    for k in range(KC):
        pixel = (c * KC + k) * coarse_size + iota((coarse_size, coarse_cols), 0)
        weight = cubic_weight(x_ms - pixel.astype(F32)).astype(BF16)
        for b in range(bands):
            row = (k * bands + b) * coarse_size
            ms_col_weight[row : row + coarse_size, b * coarse_cols : (b + 1) * coarse_cols] = weight

    def pan_to_owner(k, line):
        value = pan_part(line * 2 + y)
        pan_pair(k).wait()
        pan_owner_send[k] = (value + pan_pair_recv[k].astype(F32)).astype(BF16)
        pan_owner(k, line, z).start()

    each_line(0, pairs - 2, pan_to_owner)

    def ms_from_line(k, line):
        ms_owner(k, line, line).wait()
        ms_total[...] += ms_owner_recv[line].astype(F32)

    each_line(0, pairs - 1, ms_from_line)
    left, right = [ms_total[side, :].astype(BF16) for side in sides]
    ms_map = jnp.dot(left, ms_col_weight[0:cols, :], preferred_element_type=F32)
    ms_map = ms_map + jnp.dot(
        right, ms_col_weight[cols : 2 * cols, :], preferred_element_type=F32
    )
    values = [ms_map[:, b * coarse_cols : (b + 1) * coarse_cols] for b in range(bands)]
    synthetic = sum(synth_ref[b] * values[b] for b in range(bands))
    for b in range(bands):
        result = values[b] - gain_ref[b] * synthetic
        for k in range(bands):
            result = result + mix_ref[b, k] * values[k]
        window[half:mid, b * coarse_cols : (b + 1) * coarse_cols] = result.astype(BF16)

    has_above, has_below = m > 0, m < n - 1

    def halo_copy(k, src, rows, dst, start, row, col):
        return pltpu.make_async_remote_copy(
            src_ref=window.at[pl.ds(src, rows)],
            dst_ref=dst.at[pl.ds(start, rows)],
            send_sem=halo_ss.at[k],
            recv_sem=halo_rs.at[k],
            device_id=at(row, col),
            device_id_type=MESH,
        )

    across_copy = halo_copy(0, half, coarse_rows, beside, half, m, other)
    up_copies = [
        halo_copy(1, half, half, window, mid, m - 1, c),
        halo_copy(2, half, half, beside, mid, m - 1, other),
    ]
    down_copies = [
        halo_copy(3, coarse_rows, half, window, 0, m + 1, c),
        halo_copy(4, coarse_rows, half, beside, 0, m + 1, other),
    ]
    across_copy.start()

    @pl.when(has_above)
    def _():
        for copy in up_copies:
            copy.start()

    @pl.when(has_below)
    def _():
        for copy in down_copies:
            copy.start()

    pan_to_owner(pairs - 2, line_of(pairs - 2))
    pan_map[...] = pan_part(m)
    across_copy.wait()

    @pl.when(has_above)
    def _():
        for copy in up_copies:
            copy.wait_send()
        for copy in down_copies:
            copy.wait_recv()

    @pl.when(has_below)
    def _():
        for copy in down_copies:
            copy.wait_send()
        for copy in up_copies:
            copy.wait_recv()

    edge = jnp.zeros((half, window.shape[1]), BF16)

    @pl.when(jnp.logical_not(has_above))
    def _():
        window[0:half, :] = edge
        beside[0:half, :] = edge

    @pl.when(jnp.logical_not(has_below))
    def _():
        window[mid : mid + half, :] = edge
        beside[mid : mid + half, :] = edge

    for b in range(bands):
        lanes = slice(b * coarse_cols, (b + 1) * coarse_cols)
        across = jnp.dot(window[:, lanes], up_cols[0], preferred_element_type=F32)
        across = across + jnp.dot(beside[:, lanes], up_cols[1], preferred_element_type=F32)
        mixed[b] = jnp.dot(
            up_rows[...], across.astype(BF16), preferred_element_type=F32
        ).astype(BF16)

    store = pltpu.make_async_copy(mixed, mixed_hbm, load_sem.at[2])
    store.start()

    pan_pair(pairs - 1).wait()
    pan_map[...] += pan_pair_recv[pairs - 1].astype(F32)

    def pan_from_line(k, line):
        pan_owner(k, line, line).wait()
        pan_map[...] += pan_owner_recv[line].astype(F32)

    each_line(0, pairs - 1, pan_from_line)
    store.wait()


def local(
    pan_blocks,
    ms_blocks,
    send_list,
    tile_list,
    row_grid,
    col_grid,
    band_mix,
    band_gain,
    synth_weight,
):
    n = lax.axis_size("mrow")
    pairs = n // 2
    own_blocks, block_size, _ = pan_blocks.shape
    _, coarse_size, coarse_width = ms_blocks.shape
    slots = tile_list.shape[1]
    capacity = slots // n
    bands = band_gain.shape[0]
    pan_rows, pan_cols = KR * block_size, KC * block_size
    ms_rows, ms_cols = KR * coarse_size, KC * coarse_width
    smem = pl.BlockSpec(memory_space=pltpu.SMEM)
    vmem = pl.BlockSpec(memory_space=pltpu.VMEM)
    hbm = pl.BlockSpec(memory_space=pl.ANY)
    pan_cells, ms_cells, nodes = pl.pallas_call(
        functools.partial(cell_sums, capacity),
        grid=(n,),
        out_shape=(
            jax.ShapeDtypeStruct((n, pan_rows, pan_cols), BF16),
            jax.ShapeDtypeStruct((n, ms_rows, ms_cols), BF16),
            jax.ShapeDtypeStruct((8, 128), F32),
        ),
        in_specs=[smem, vmem, vmem, vmem, vmem],
        out_specs=(
            pl.BlockSpec((1, pan_rows, pan_cols), lambda t: (t, 0, 0)),
            pl.BlockSpec((1, ms_rows, ms_cols), lambda t: (t, 0, 0)),
            pl.BlockSpec((8, 128), lambda t: (0, 0)),
        ),
        scratch_shapes=[
            pltpu.SMEM((n * KR * KC,), jnp.int32),
            pltpu.SMEM((own_blocks,), jnp.int32),
        ],
        name="cell_sums",
    )(send_list, pan_blocks, ms_blocks, row_grid[None, :], col_grid)

    coarse_rows, coarse_cols = TR // 4, TC // 4
    dma = pltpu.SemaphoreType.DMA
    ms_slots = pltpu.VMEM((pairs, 2 * coarse_rows, pan_cols), BF16)
    pan_slots = pltpu.VMEM((pairs, TR, TC), BF16)
    mixed, pan_map = pl.pallas_call(
        functools.partial(mapping, col_grid.shape[1]),
        out_shape=(
            jax.ShapeDtypeStruct((bands, TR, TC), BF16),
            jax.ShapeDtypeStruct((TR, TC), F32),
        ),
        in_specs=[vmem, hbm, hbm, smem, smem, smem],
        out_specs=(hbm, vmem),
        scratch_shapes=[
            pltpu.VMEM((n, pan_rows, pan_cols), BF16),
            pltpu.VMEM((n, ms_rows, ms_cols), BF16),
            pltpu.VMEM((2, n, 8, 128), F32),
            ms_slots,
            ms_slots,
            ms_slots,
            ms_slots,
            pan_slots,
            pan_slots,
            pan_slots,
            pan_slots,
            pltpu.VMEM((2 * coarse_rows, pan_cols), F32),
            pltpu.VMEM((pan_cols, TC), BF16),
            pltpu.VMEM((ms_cols, bands * coarse_cols), BF16),
            pltpu.VMEM((2 * coarse_rows, bands * coarse_cols), BF16),
            pltpu.VMEM((2 * coarse_rows, bands * coarse_cols), BF16),
            pltpu.VMEM((2, coarse_cols, TC), BF16),
            pltpu.VMEM((TR, 2 * coarse_rows), BF16),
            pltpu.VMEM((bands, TR, TC), BF16),
            dma((3,)),
            dma((2, n)),
            dma((2, n)),
        ]
        + [dma((pairs,))] * 8
        + [dma((5,)), dma((5,))],
        compiler_params=pltpu.CompilerParams(
            collective_id=0, has_side_effects=True, vmem_limit_bytes=60 * 1024 * 1024
        ),
        name="mapping",
    )(nodes, pan_cells, ms_cells, band_mix, band_gain, synth_weight)
    detail = band_gain[:, None, None] * pan_map[None]
    return (mixed.astype(F32) + detail).astype(BF16)


def solution(mesh):
    return jax.shard_map(
        local,
        mesh=mesh,
        in_specs=(
            P(("scene", "mrow", "mcol"), None, None),
            P(("scene", "mrow", "mcol"), None, None),
            P(None, ("scene", "mrow", "mcol")),
            P(None, ("scene", "mrow", "mcol")),
            P(("scene", "mrow")),
            P(("scene", "mrow"), "mcol"),
            P(),
            P(),
            P(),
        ),
        out_specs=P(None, ("scene", "mrow"), "mcol"),
        check_vma=False,
    )
```

```python
import functools

import jax
import jax.numpy as jnp
from jax import lax
from jax.experimental import pallas as pl
from jax.experimental.pallas import tpu as pltpu
from jax.sharding import PartitionSpec as P

GRID = 64
TR = 128
TC = 512
KR = 2
KC = 5
MESH = pl.DeviceIdType.MESH
F32 = jnp.float32
BF16 = jnp.bfloat16


def cubic_weight(offset):
    outer = jnp.maximum(2.0 - jnp.abs(offset), 0.0)
    shifted = outer - 1.0
    inner = jnp.maximum(shifted, 0.0)
    return outer * outer * (0.5 * shifted) + inner * inner * (1.0 - 2.0 * inner)


def iota(shape, dim):
    return lax.broadcasted_iota(jnp.int32, shape, dim)


def cell_sums(
    capacity,
    send_ref,
    pan_hbm,
    ms_hbm,
    row_ref,
    col_ref,
    pan_out,
    ms_out,
    nodes_out,
    first_block,
    next_block,
    pan_ref,
    ms_ref,
    load_sem,
):
    tile = pl.program_id(0)
    own_blocks, block_size, _ = pan_ref.shape
    _, coarse_size, coarse_width = ms_ref.shape
    first_col = lax.axis_index("mcol") * KC

    @pl.when(tile == 0)
    def _():
        pan_load = pltpu.make_async_copy(pan_hbm, pan_ref, load_sem.at[0])
        ms_load = pltpu.make_async_copy(ms_hbm, ms_ref, load_sem.at[1])
        pan_load.start()
        ms_load.start()
        nodes_out[...] = jnp.zeros_like(nodes_out)
        nodes_out[0:1, 0 : row_ref.shape[1]] = row_ref[...]
        nodes_out[1:2, 0 : col_ref.shape[1]] = col_ref[...]

        def clear(k, carry):
            for r in range(KR * KC):
                first_block[k * (KR * KC) + r] = -1
            return carry

        lax.fori_loop(0, first_block.shape[0] // (KR * KC), clear, 0)

        def enter(block, carry):
            cell = (send_ref[0, block] // capacity * KR + send_ref[1, block]) * KC
            cell = cell + send_ref[2, block] - first_col
            next_block[block] = first_block[cell]
            first_block[cell] = block
            return carry

        lax.fori_loop(0, own_blocks, enter, 0, unroll=4)
        pan_load.wait()
        ms_load.wait()

    for row in range(KR):
        for col in range(KC):

            def add(carry):
                block, pan, ms = carry
                pan = pan + pan_ref[block].astype(F32)
                ms = ms + ms_ref[block].astype(F32)
                return next_block[block], pan, ms

            start = (
                first_block[(tile * KR + row) * KC + col],
                jnp.zeros((block_size, block_size), F32),
                jnp.zeros((coarse_size, coarse_width), F32),
            )
            _, pan, ms = lax.while_loop(lambda carry: carry[0] >= 0, add, start)
            rows = slice(row * block_size, (row + 1) * block_size)
            pan_out[0, rows, col * block_size : (col + 1) * block_size] = pan.astype(BF16)
            rows = slice(row * coarse_size, (row + 1) * coarse_size)
            ms_out[0, rows, col * coarse_width : (col + 1) * coarse_width] = ms.astype(BF16)


def row_coord(nodes, position, offset):
    first = position < GRID
    a = jnp.where(first, nodes[0:1, 0:1], nodes[0:1, 1:2])
    b = jnp.where(first, nodes[0:1, 1:2], nodes[0:1, 2:3])
    within = (jnp.where(first, position, position - GRID).astype(F32) + offset) / GRID
    return a + (b - a) * within


def col_coord(nodes, after, is_last, count, position, offset):
    segment = position // GRID
    coord = jnp.zeros(position.shape, F32)
    for s in range(count):
        left, shift = nodes[1:2, s : s + 1], s * GRID
        if s + 1 < count:
            right = nodes[1:2, s + 1 : s + 2]
        else:
            right = jnp.where(is_last, left, after)
            left = jnp.where(is_last, nodes[1:2, s - 1 : s], left)
            shift = jnp.where(is_last, shift - GRID, shift)
        within = ((position - shift).astype(F32) + offset) / GRID
        coord = jnp.where(segment == s, left + (right - left) * within, coord)
    return coord


def mapping(
    col_nodes,
    nodes_ref,
    pan_hbm,
    ms_hbm,
    mix_ref,
    gain_ref,
    synth_ref,
    mixed_hbm,
    pan_map,
    pan_ref,
    ms_ref,
    nodes_all,
    ms_pair_send,
    ms_pair_recv,
    ms_owner_send,
    ms_owner_recv,
    pan_pair_send,
    pan_pair_recv,
    pan_owner_send,
    pan_owner_recv,
    ms_total,
    col_weight,
    ms_col_weight,
    window,
    beside,
    up_cols,
    up_rows,
    mixed,
    load_sem,
    nodes_ss,
    nodes_rs,
    ms_pair_ss,
    ms_pair_rs,
    ms_owner_ss,
    ms_owner_rs,
    pan_pair_ss,
    pan_pair_rs,
    pan_owner_ss,
    pan_owner_rs,
    halo_ss,
    halo_rs,
):
    n = lax.axis_size("mrow")
    pairs = n // 2
    scene = lax.axis_index("scene")
    m = lax.axis_index("mrow")
    c = lax.axis_index("mcol")
    z, y = m // 2, m % 2
    twin = z * 2 + (1 - y)
    other = 1 - c
    cols = pan_ref.shape[2]
    pan_rows = pan_ref.shape[1]
    ms_rows = ms_ref.shape[1]
    bands = mixed.shape[0]
    coarse_rows = TR // 4
    coarse_cols = TC // 4
    half = coarse_rows // 2
    mid = half + coarse_rows
    coarse_size = ms_rows // KR
    is_last = c == lax.axis_size("mcol") - 1

    def at(row, col):
        return (scene, row, col)

    def line_of(k):
        return lax.rem(z + 1 + lax.rem(pairs // 2 - 1 + k, pairs - 1), pairs)

    barrier = pltpu.get_barrier_semaphore()

    def greet(k, carry):
        row = lax.rem(m + k, n)
        pl.semaphore_signal(barrier, inc=1, device_id=at(row, c), device_id_type=MESH)
        pl.semaphore_signal(barrier, inc=1, device_id=at(row, other), device_id_type=MESH)
        return carry

    pl.semaphore_signal(barrier, inc=1, device_id=at(m, other), device_id_type=MESH)
    lax.fori_loop(1, n, greet, 0)
    ms_load = pltpu.make_async_copy(ms_hbm, ms_ref, load_sem.at[0])
    pan_load = pltpu.make_async_copy(pan_hbm, pan_ref, load_sem.at[1])
    ms_load.start()
    pan_load.start()

    tap = iota((TR, 2 * coarse_rows), 1) - (half - 2)
    spot = (iota((TR, 2 * coarse_rows), 0).astype(F32) - 1.5) * 0.25 + 2.0
    up_rows[...] = cubic_weight(spot - tap.astype(F32)).astype(BF16)
    ms_col_weight[...] = jnp.zeros_like(ms_col_weight)
    pl.semaphore_wait(barrier, 2 * n - 1)

    def nodes_copy(slot_row, slot_col, row, col):
        return pltpu.make_async_remote_copy(
            src_ref=nodes_ref,
            dst_ref=nodes_all.at[slot_col, slot_row],
            send_sem=nodes_ss.at[col, row],
            recv_sem=nodes_rs.at[slot_col, slot_row],
            device_id=at(row, col),
            device_id_type=MESH,
        )

    def send_nodes(k, carry):
        row = lax.rem(m + k, n)
        nodes_copy(m, c, row, c).start()
        nodes_copy(m, c, row, other).start()
        return carry

    lax.fori_loop(1, n, send_nodes, 0)
    nodes_copy(m, c, m, other).start()
    nodes_all[c, m] = nodes_ref[...]

    spot = (iota((coarse_cols, TC), 1).astype(F32) - 1.5) * 0.25 + 2.0
    tap = iota((coarse_cols, TC), 0) + 2
    up_cols[0] = cubic_weight(spot - tap.astype(F32)).astype(BF16)
    tap = tap + jnp.where(c == 0, coarse_cols, -coarse_cols)
    up_cols[1] = cubic_weight(spot - tap.astype(F32)).astype(BF16)
    ms_load.wait()

    def wait_nodes(k, carry):
        row = lax.rem(m + k, n)
        nodes_copy(row, c, row, c).wait()
        nodes_copy(row, other, row, other).wait()
        return carry

    lax.fori_loop(1, n, wait_nodes, 0)
    nodes_copy(m, other, m, other).wait()

    sides = (slice(0, coarse_rows), slice(coarse_rows, 2 * coarse_rows))

    def ms_part(tile):
        nodes = nodes_all[c, tile]
        shape = (coarse_rows, ms_rows)
        spots = (row_coord(nodes, 4 * iota(shape, 0) + 1, 0.5) - 1.5) * 0.25
        weight = cubic_weight(spots - iota(shape, 1).astype(F32)).astype(BF16)
        left = jnp.dot(weight, ms_ref[tile, :, 0:cols], preferred_element_type=F32)
        right = jnp.dot(weight, ms_ref[tile, :, cols : 2 * cols], preferred_element_type=F32)
        return left, right

    def pan_part(tile):
        nodes = nodes_all[c, tile]
        after = nodes_all[1, tile][1:2, 0:1]
        x_pan = col_coord(nodes, after, is_last, col_nodes, iota((1, TC), 1), 0.0)
        size = cols // KC
        for k in range(KC):
            pixel = (c * KC + k) * size + iota((size, TC), 0)
            col_weight[k * size : (k + 1) * size, :] = cubic_weight(
                x_pan - pixel.astype(F32)
            ).astype(BF16)
        shape = (TR, pan_rows)
        weight = cubic_weight(
            row_coord(nodes, iota(shape, 0), 0.0) - iota(shape, 1).astype(F32)
        ).astype(BF16)
        rows = jnp.dot(weight, pan_ref[tile], preferred_element_type=F32)
        return jnp.dot(rows.astype(BF16), col_weight[...], preferred_element_type=F32)

    def pair_copy(send, recv, ss, rs, k):
        return pltpu.make_async_remote_copy(
            src_ref=send.at[k],
            dst_ref=recv.at[k],
            send_sem=ss.at[k],
            recv_sem=rs.at[k],
            device_id=at(twin, c),
            device_id_type=MESH,
        )

    def owner_copy(send, recv, ss, rs, k, line, slot):
        return pltpu.make_async_remote_copy(
            src_ref=send.at[k],
            dst_ref=recv.at[slot],
            send_sem=ss.at[k],
            recv_sem=rs.at[slot],
            device_id=at(line * 2 + y, c),
            device_id_type=MESH,
        )

    ms_pair = functools.partial(pair_copy, ms_pair_send, ms_pair_recv, ms_pair_ss, ms_pair_rs)
    pan_pair = functools.partial(pair_copy, pan_pair_send, pan_pair_recv, pan_pair_ss, pan_pair_rs)
    ms_owner = functools.partial(
        owner_copy, ms_owner_send, ms_owner_recv, ms_owner_ss, ms_owner_rs
    )
    pan_owner = functools.partial(
        owner_copy, pan_owner_send, pan_owner_recv, pan_owner_ss, pan_owner_rs
    )

    def ms_to_twin(k, tile):
        for side, value in zip(sides, ms_part(tile)):
            ms_pair_send[k, side, :] = value.astype(BF16)
        ms_pair(k).start()

    def pan_to_twin(k, tile):
        pan_pair_send[k] = pan_part(tile).astype(BF16)
        pan_pair(k).start()

    def each_line(first, last, step):
        def body(k, carry):
            step(k, line_of(k))
            return carry

        lax.fori_loop(first, last, body, 0)

    each_line(0, pairs - 1, lambda k, line: ms_to_twin(k, line * 2 + 1 - y))
    ms_to_twin(pairs - 1, twin)
    pan_load.wait()
    each_line(0, pairs - 1, lambda k, line: pan_to_twin(k, line * 2 + 1 - y))
    pan_to_twin(pairs - 1, twin)

    def ms_to_owner(k, line):
        values = ms_part(line * 2 + y)
        ms_pair(k).wait()
        for side, value in zip(sides, values):
            ms_owner_send[k, side, :] = (value + ms_pair_recv[k, side, :].astype(F32)).astype(BF16)
        ms_owner(k, line, z).start()

    each_line(0, pairs - 1, ms_to_owner)
    values = ms_part(m)
    ms_pair(pairs - 1).wait()
    for side, value in zip(sides, values):
        ms_total[side, :] = value + ms_pair_recv[pairs - 1, side, :].astype(F32)

    x_ms = col_coord(
        nodes_ref[...],
        nodes_all[1, m][1:2, 0:1],
        is_last,
        col_nodes,
        4 * iota((1, coarse_cols), 1) + 1,
        0.5,
    )
    x_ms = (x_ms - 1.5) * 0.25
    for k in range(KC):
        pixel = (c * KC + k) * coarse_size + iota((coarse_size, coarse_cols), 0)
        weight = cubic_weight(x_ms - pixel.astype(F32)).astype(BF16)
        for b in range(bands):
            row = (k * bands + b) * coarse_size
            ms_col_weight[row : row + coarse_size, b * coarse_cols : (b + 1) * coarse_cols] = weight

    def pan_to_owner(k, line):
        value = pan_part(line * 2 + y)
        pan_pair(k).wait()
        pan_owner_send[k] = (value + pan_pair_recv[k].astype(F32)).astype(BF16)
        pan_owner(k, line, z).start()

    each_line(0, pairs - 2, pan_to_owner)

    def ms_from_line(k, line):
        ms_owner(k, line, line).wait()
        ms_total[...] += ms_owner_recv[line].astype(F32)

    each_line(0, pairs - 1, ms_from_line)
    left, right = [ms_total[side, :].astype(BF16) for side in sides]
    ms_map = jnp.dot(left, ms_col_weight[0:cols, :], preferred_element_type=F32)
    ms_map = ms_map + jnp.dot(
        right, ms_col_weight[cols : 2 * cols, :], preferred_element_type=F32
    )
    values = [ms_map[:, b * coarse_cols : (b + 1) * coarse_cols] for b in range(bands)]
    synthetic = sum(synth_ref[b] * values[b] for b in range(bands))
    for b in range(bands):
        result = values[b] - gain_ref[b] * synthetic
        for k in range(bands):
            result = result + mix_ref[b, k] * values[k]
        window[half:mid, b * coarse_cols : (b + 1) * coarse_cols] = result.astype(BF16)

    has_above, has_below = m > 0, m < n - 1

    def halo_copy(k, src, rows, dst, start, row, col):
        return pltpu.make_async_remote_copy(
            src_ref=window.at[pl.ds(src, rows)],
            dst_ref=dst.at[pl.ds(start, rows)],
            send_sem=halo_ss.at[k],
            recv_sem=halo_rs.at[k],
            device_id=at(row, col),
            device_id_type=MESH,
        )

    across_copy = halo_copy(0, half, coarse_rows, beside, half, m, other)
    up_copies = [
        halo_copy(1, half, half, window, mid, m - 1, c),
        halo_copy(2, half, half, beside, mid, m - 1, other),
    ]
    down_copies = [
        halo_copy(3, coarse_rows, half, window, 0, m + 1, c),
        halo_copy(4, coarse_rows, half, beside, 0, m + 1, other),
    ]
    across_copy.start()

    @pl.when(has_above)
    def _():
        for copy in up_copies:
            copy.start()

    @pl.when(has_below)
    def _():
        for copy in down_copies:
            copy.start()

    pan_to_owner(pairs - 2, line_of(pairs - 2))
    pan_map[...] = pan_part(m)
    across_copy.wait()

    @pl.when(has_above)
    def _():
        for copy in up_copies:
            copy.wait_send()
        for copy in down_copies:
            copy.wait_recv()

    @pl.when(has_below)
    def _():
        for copy in down_copies:
            copy.wait_send()
        for copy in up_copies:
            copy.wait_recv()

    edge = jnp.zeros((half, window.shape[1]), BF16)

    @pl.when(jnp.logical_not(has_above))
    def _():
        window[0:half, :] = edge
        beside[0:half, :] = edge

    @pl.when(jnp.logical_not(has_below))
    def _():
        window[mid : mid + half, :] = edge
        beside[mid : mid + half, :] = edge

    for b in range(bands):
        lanes = slice(b * coarse_cols, (b + 1) * coarse_cols)
        across = jnp.dot(window[:, lanes], up_cols[0], preferred_element_type=F32)
        across = across + jnp.dot(beside[:, lanes], up_cols[1], preferred_element_type=F32)
        mixed[b] = jnp.dot(
            up_rows[...], across.astype(BF16), preferred_element_type=F32
        ).astype(BF16)

    store = pltpu.make_async_copy(mixed, mixed_hbm, load_sem.at[2])
    store.start()

    pan_pair(pairs - 1).wait()
    pan_map[...] += pan_pair_recv[pairs - 1].astype(F32)

    def pan_from_line(k, line):
        pan_owner(k, line, line).wait()
        pan_map[...] += pan_owner_recv[line].astype(F32)

    each_line(0, pairs - 1, pan_from_line)
    store.wait()


def local(
    pan_blocks,
    ms_blocks,
    send_list,
    tile_list,
    row_grid,
    col_grid,
    band_mix,
    band_gain,
    synth_weight,
):
    n = lax.axis_size("mrow")
    pairs = n // 2
    own_blocks, block_size, _ = pan_blocks.shape
    _, coarse_size, coarse_width = ms_blocks.shape
    slots = tile_list.shape[1]
    capacity = slots // n
    bands = band_gain.shape[0]
    pan_rows, pan_cols = KR * block_size, KC * block_size
    ms_rows, ms_cols = KR * coarse_size, KC * coarse_width
    smem = pl.BlockSpec(memory_space=pltpu.SMEM)
    vmem = pl.BlockSpec(memory_space=pltpu.VMEM)
    hbm = pl.BlockSpec(memory_space=pl.ANY)
    pan_cells, ms_cells, nodes = pl.pallas_call(
        functools.partial(cell_sums, capacity),
        grid=(n,),
        out_shape=(
            jax.ShapeDtypeStruct((n, pan_rows, pan_cols), BF16),
            jax.ShapeDtypeStruct((n, ms_rows, ms_cols), BF16),
            jax.ShapeDtypeStruct((8, 128), F32),
        ),
        in_specs=[smem, hbm, hbm, vmem, vmem],
        out_specs=(
            pl.BlockSpec((1, pan_rows, pan_cols), lambda t: (t, 0, 0)),
            pl.BlockSpec((1, ms_rows, ms_cols), lambda t: (t, 0, 0)),
            pl.BlockSpec((8, 128), lambda t: (0, 0)),
        ),
        scratch_shapes=[
            pltpu.SMEM((n * KR * KC,), jnp.int32),
            pltpu.SMEM((own_blocks,), jnp.int32),
            pltpu.VMEM(pan_blocks.shape, BF16),
            pltpu.VMEM(ms_blocks.shape, BF16),
            pltpu.SemaphoreType.DMA((2,)),
        ],
        name="cell_sums",
    )(send_list, pan_blocks, ms_blocks, row_grid[None, :], col_grid)

    coarse_rows, coarse_cols = TR // 4, TC // 4
    dma = pltpu.SemaphoreType.DMA
    ms_slots = pltpu.VMEM((pairs, 2 * coarse_rows, pan_cols), BF16)
    pan_slots = pltpu.VMEM((pairs, TR, TC), BF16)
    mixed, pan_map = pl.pallas_call(
        functools.partial(mapping, col_grid.shape[1]),
        out_shape=(
            jax.ShapeDtypeStruct((bands, TR, TC), BF16),
            jax.ShapeDtypeStruct((TR, TC), F32),
        ),
        in_specs=[vmem, hbm, hbm, smem, smem, smem],
        out_specs=(hbm, vmem),
        scratch_shapes=[
            pltpu.VMEM((n, pan_rows, pan_cols), BF16),
            pltpu.VMEM((n, ms_rows, ms_cols), BF16),
            pltpu.VMEM((2, n, 8, 128), F32),
            ms_slots,
            ms_slots,
            ms_slots,
            ms_slots,
            pan_slots,
            pan_slots,
            pan_slots,
            pan_slots,
            pltpu.VMEM((2 * coarse_rows, pan_cols), F32),
            pltpu.VMEM((pan_cols, TC), BF16),
            pltpu.VMEM((ms_cols, bands * coarse_cols), BF16),
            pltpu.VMEM((2 * coarse_rows, bands * coarse_cols), BF16),
            pltpu.VMEM((2 * coarse_rows, bands * coarse_cols), BF16),
            pltpu.VMEM((2, coarse_cols, TC), BF16),
            pltpu.VMEM((TR, 2 * coarse_rows), BF16),
            pltpu.VMEM((bands, TR, TC), BF16),
            dma((3,)),
            dma((2, n)),
            dma((2, n)),
        ]
        + [dma((pairs,))] * 8
        + [dma((5,)), dma((5,))],
        compiler_params=pltpu.CompilerParams(
            collective_id=0, has_side_effects=True, vmem_limit_bytes=60 * 1024 * 1024
        ),
        name="mapping",
    )(nodes, pan_cells, ms_cells, band_mix, band_gain, synth_weight)
    detail = band_gain[:, None, None] * pan_map[None]
    return (mixed.astype(F32) + detail).astype(BF16)


def solution(mesh):
    return jax.shard_map(
        local,
        mesh=mesh,
        in_specs=(
            P(("scene", "mrow", "mcol"), None, None),
            P(("scene", "mrow", "mcol"), None, None),
            P(None, ("scene", "mrow", "mcol")),
            P(None, ("scene", "mrow", "mcol")),
            P(("scene", "mrow")),
            P(("scene", "mrow"), "mcol"),
            P(),
            P(),
            P(),
        ),
        out_specs=P(None, ("scene", "mrow"), "mcol"),
        check_vma=False,
    )
```
